256 devices in a mesh: tile: 16 (over x, y), tm: 16 (over z, core).
Axes of the slice: x: 4, y: 4, z: 8, core: 2. Of those that a mesh axis runs over, the one named last changes fastest.
Arguments:
- histories: bfloat16 [16, 64, 128, 1024], P('tile', 'tm'), may hold values from -6 to 6
- gain_time: float32 [1024], replicated, may hold values from 0.25 to 1.75
- wq_time: bfloat16 [1024, 1024], replicated
- wkv_time: bfloat16 [1024, 512], replicated
- wo_time: bfloat16 [1024, 1024], replicated, may hold values from -0.1875 to 0.1875
- gain_space: float32 [1024], replicated, may hold values from 0.25 to 1.75
- wq_space: bfloat16 [1024, 1024], replicated
- wkv_space: bfloat16 [1024, 512], replicated
- wo_space: bfloat16 [1024, 1024], replicated, may hold values from -0.1875 to 0.1875
- neighbours: int32 [16, 8], P('tile'), may hold values from 0 to 15, as said below
- nbr_valid: int32 [16, 8], P('tile'), may hold values from 0 to 1, as said below
- agent_valid: int32 [16, 64], P('tile'), may hold values from 0 to 1
Outputs:
- updated: bfloat16 [16, 64, 128, 1024], P('tile', 'tm')
The draws below stay inside these ranges and needn't reach their ends.
Inputs may be any that keep to these rules, and one draw needn't show every extreme that they name: `neighbours`: row i starts with tile i; the entries of a row are distinct tiles. `nbr_valid`: the first entry of every row is 1; row 0 is all ones; other rows keep differing shares of their entries.
All inputs are finite; a program needn't handle non-finite values.
Results may differ from the reference program's by a relative error of at most 0.014.
The reference program's roundings to bfloat16 on the way count: a program that leaves them out, or rounds other values in their place, can miss the bound.
Values may be sent and summed in bfloat16 or wider, within the bound.
A program may use at most 128 MiB of HBM per device.

```python
import jax
import jax.numpy as jnp
from jax import lax

D = 1024
HEADS = 16
KV_HEADS = 4
HEAD_DIM = 64
STEPS = 128
AGENTS = 64
TILES = 16
NBRS = 8


def attention_pair(key):
    key_query, key_keys, key_values = jax.random.split(key, 3)
    width_kv = KV_HEADS * HEAD_DIM
    w_query = jax.random.normal(key_query, (D, D), jnp.float32) * D ** (-0.5)
    w_keys = jax.random.normal(key_keys, (D, width_kv), jnp.float32) * D ** (-0.5)
    w_values = jax.random.normal(key_values, (D, width_kv), jnp.float32) * D ** (-0.5)
    return (w_query, jnp.concatenate([w_keys, w_values], axis=1))


def draw_wq_time(key, part):
    return attention_pair(jax.random.fold_in(key, 101))[0].astype(jnp.bfloat16)


def draw_wkv_time(key, part):
    return attention_pair(jax.random.fold_in(key, 101))[1].astype(jnp.bfloat16)


def draw_wq_space(key, part):
    return attention_pair(jax.random.fold_in(key, 202))[0].astype(jnp.bfloat16)


def draw_wkv_space(key, part):
    return attention_pair(jax.random.fold_in(key, 202))[1].astype(jnp.bfloat16)


def draw_neighbours(key, part):
    base = jax.random.fold_in(key, 303)

    def one_row(row_key, tile_number):
        order = jax.random.permutation(row_key, TILES - 1).astype(jnp.int32)
        other_tiles = (tile_number + 1 + order) % TILES
        return jnp.concatenate([tile_number[None], other_tiles[:NBRS - 1]])
    row_keys = jax.random.split(base, TILES)
    return jax.vmap(one_row)(row_keys, jnp.arange(TILES, dtype=jnp.int32)).astype(jnp.int32)


def draw_nbr_valid(key, part):
    key_level, key_flags = jax.random.split(jax.random.fold_in(key, 404))
    level = jax.random.randint(key_level, (TILES, 1), 1, 5)
    flags = jax.random.randint(key_flags, (TILES, NBRS), 0, 4) < level
    column = jnp.arange(NBRS)[None, :] == 0
    first_row = jnp.arange(TILES)[:, None] == 0
    return (flags | column | first_row).astype(jnp.int32)


def draw_agent_valid(key, part):
    flags = jax.random.randint(jax.random.fold_in(key, 505), (TILES, AGENTS), 0, 4) > 0
    column = jnp.arange(AGENTS)[None, :] == 0
    return (flags | column).astype(jnp.int32)


def block_scale(own_key, shape, pieces, low, largest):
    level, own = 1.0, jax.random.fold_in(own_key, 6)
    for axis_at, blocks in pieces:
        steps = jnp.exp(jax.random.uniform(jax.random.fold_in(own, axis_at), (blocks,), jnp.float32, low / len(pieces), largest / len(pieces)))
        level = level * jnp.repeat(steps, shape[axis_at] // blocks).reshape([-1 if axis == axis_at else 1 for axis in range(len(shape))])
    return level


def gaussian(own_key, dims, width, limit, pieces=(), kind=jnp.bfloat16):
    array = jax.random.normal(own_key, dims, jnp.float32) * width
    if len(pieces) > 0:
        array = block_scale(own_key, dims, pieces, -0.22, 0.18) * array
    return jnp.clip(array, min=-limit, max=limit).astype(kind)


def setup_inputs(seed: int = 0) -> dict:
    arg_keys = jax.random.split(jax.random.key(seed), 13)
    return {
        "histories": gaussian(arg_keys[0], (TILES, AGENTS, STEPS, D), 1.0, 6.0, ((0, 16), (1, 16))),
        "gain_time": jnp.clip(1.0 + 0.15 * jax.random.normal(arg_keys[1], (D,), jnp.float32), 0.25, 1.75),
        "wq_time": draw_wq_time(jax.random.fold_in(arg_keys[12], 71), 0),
        "wkv_time": draw_wkv_time(jax.random.fold_in(arg_keys[12], 71), 0),
        "wo_time": gaussian(arg_keys[4], (D, D), D ** -0.5, 0.1875),
        "gain_space": jnp.clip(1.0 + 0.15 * jax.random.normal(arg_keys[5], (D,), jnp.float32), 0.25, 1.75),
        "wq_space": draw_wq_space(jax.random.fold_in(arg_keys[12], 71), 0),
        "wkv_space": draw_wkv_space(jax.random.fold_in(arg_keys[12], 71), 0),
        "wo_space": gaussian(arg_keys[8], (D, D), D ** -0.5, 0.1875),
        "neighbours": draw_neighbours(jax.random.fold_in(arg_keys[12], 71), 0),
        "nbr_valid": draw_nbr_valid(jax.random.fold_in(arg_keys[12], 71), 0),
        "agent_valid": draw_agent_valid(jax.random.fold_in(arg_keys[12], 71), 0),
    }


def norm_rows(values, gain):
    wide = values.astype(jnp.float32)
    meansq = lax.optimization_barrier(jnp.mean(wide * wide, axis=-1, keepdims=True))
    return (wide * lax.rsqrt(meansq + 1e-05) * gain.astype(jnp.float32)).astype(jnp.bfloat16)

def temporal_block(history, gain, w_query, w_keyval, w_out):
    batch, nsteps, model_width = history.shape
    groups = HEADS // KV_HEADS
    normed = norm_rows(history, gain).reshape(batch * nsteps, model_width)
    queries = jnp.dot(normed, w_query, preferred_element_type=jnp.float32).astype(jnp.bfloat16)
    queries = queries.reshape(batch, nsteps, KV_HEADS, groups, HEAD_DIM)
    keyval = jnp.dot(normed, w_keyval, preferred_element_type=jnp.float32).astype(jnp.bfloat16)
    keyval = keyval.reshape(batch, nsteps, 2, KV_HEADS, HEAD_DIM)
    logit_scores = jnp.einsum('bskgd,btkd->bkgst', queries.astype(jnp.float32), keyval[:, :, 0].astype(jnp.float32))
    logit_scores = logit_scores * HEAD_DIM ** (-0.5)
    causal = jnp.arange(nsteps)[:, None] >= jnp.arange(nsteps)[None, :]
    logit_scores = jnp.where(causal, logit_scores, -1e+30)
    row_top = lax.optimization_barrier(jnp.max(logit_scores, axis=-1, keepdims=True))
    expd = jnp.where(causal, jnp.exp(logit_scores - row_top), 0.0)
    probs = (expd / lax.optimization_barrier(jnp.sum(expd, axis=-1, keepdims=True))).astype(jnp.bfloat16)
    mixed = jnp.einsum('bkgst,btkd->bskgd', probs.astype(jnp.float32), keyval[:, :, 1].astype(jnp.float32))
    mixed = mixed.astype(jnp.bfloat16).reshape(batch * nsteps, model_width)
    projected = jnp.dot(mixed, w_out, preferred_element_type=jnp.float32)
    return (history.astype(jnp.float32) + projected.reshape(batch, nsteps, model_width)).astype(jnp.bfloat16)

def reference(histories, gain_time, wq_time, wkv_time, wo_time, gain_space, wq_space, wkv_space, wo_space, neighbours, nbr_valid, agent_valid):
    groups = HEADS // KV_HEADS
    time_mixed = lax.map(lambda block: temporal_block(block, gain_time, wq_time, wkv_time, wo_time), histories)
    normed = norm_rows(time_mixed, gain_space)
    flat = normed.reshape(-1, D)
    queries = jnp.dot(flat, wq_space, preferred_element_type=jnp.float32).astype(jnp.bfloat16)
    queries = queries.reshape(TILES, AGENTS, STEPS, KV_HEADS, groups, HEAD_DIM)
    key_values = jnp.dot(flat, wkv_space, preferred_element_type=jnp.float32).astype(jnp.bfloat16)
    key_values = key_values.reshape(TILES, AGENTS, STEPS, 2 * KV_HEADS * HEAD_DIM)
    alive_mask = agent_valid.astype(jnp.float32)

    def one_tile(scan_item):
        tile_queries, tile_list, tile_valid, tile_state = scan_item
        chosen = key_values[tile_list]
        key_weight = (tile_valid.astype(jnp.float32)[:, None] * alive_mask[tile_list]).reshape(-1)
        chosen = jnp.transpose(chosen, (2, 0, 1, 3)).reshape(STEPS, NBRS * AGENTS, 2, KV_HEADS, HEAD_DIM)
        step_queries = jnp.transpose(tile_queries, (1, 0, 2, 3, 4))

        def one_step(paired):
            current_query, current_keyvalue = paired
            logit_scores = jnp.einsum('nfqe,yfe->fqny', current_query.astype(jnp.float32), current_keyvalue[:, 0].astype(jnp.float32))
            logit_scores = logit_scores * HEAD_DIM ** (-0.5)
            logit_scores = jnp.where(key_weight > 0, logit_scores, -1e+30)
            row_top = lax.optimization_barrier(jnp.max(logit_scores, axis=-1, keepdims=True))
            weights = jnp.exp(logit_scores - row_top) * key_weight
            rounded_result = lax.optimization_barrier(weights.astype(jnp.bfloat16)).astype(jnp.float32)
            summed_values = jnp.einsum('zxrv,vzc->rzxc', rounded_result, current_keyvalue[:, 1].astype(jnp.float32))
            denominator = jnp.transpose(lax.optimization_barrier(jnp.sum(weights, axis=-1)), (2, 0, 1))
            return (summed_values / denominator[..., None]).astype(jnp.bfloat16)
        mixed = lax.map(one_step, (step_queries, chosen))
        mixed = jnp.transpose(mixed, (1, 0, 2, 3, 4)).reshape(AGENTS * STEPS, D)
        projected = jnp.dot(mixed, wo_space, preferred_element_type=jnp.float32)
        return (tile_state.astype(jnp.float32) + projected.reshape(AGENTS, STEPS, D)).astype(jnp.bfloat16)
    return lax.map(one_tile, (queries, neighbours, nbr_valid, time_mixed))
```

```python
import functools

import jax
import jax.numpy as jnp
from jax import lax
from jax.experimental import pallas as pl
from jax.experimental.pallas import tpu as pltpu
from jax.sharding import PartitionSpec as P

HEADS = 16
KV_HEADS = 4
HEAD_DIM = 64
D = 1024
LANES = 128
QTILES = D // LANES
MESH = pl.DeviceIdType.MESH
BF16 = jnp.bfloat16
F32 = jnp.float32
CHUNKS = 2
PHASES = 4
NEG = -1e30


def normalize(wide, gain):
    meansq = jnp.mean(wide * wide, axis=-1, keepdims=True)
    return (wide * lax.rsqrt(meansq + 1e-05) * gain).astype(BF16)


def mm(a, b):
    return jnp.dot(a, b, preferred_element_type=F32)


def mm_t(a, b):
    return lax.dot_general(a, b, (((1,), (1,)), ((), ())), preferred_element_type=F32)


def low_lanes(rows):
    return lax.broadcasted_iota(jnp.int32, (rows, LANES), 1) < HEAD_DIM


def swap_halves(x):
    return pltpu.roll(x, HEAD_DIM, 1)


def pack_keyval(kv, k):
    at = (k // 2) * LANES
    keys = kv[:, at : at + LANES]
    values = kv[:, 2 * LANES + at : 3 * LANES + at]
    low = low_lanes(kv.shape[0])
    if k % 2 == 0:
        return jnp.where(low, keys, swap_halves(values))
    return jnp.where(low, swap_halves(keys), values)


def stack_queries(block):
    low = low_lanes(block.shape[0])
    parts = []
    for pair in range(2):
        half = block[:, pair * LANES : (pair + 1) * LANES] * 0.125
        parts.append(jnp.where(low, half, 0.0))
        parts.append(jnp.where(low, swap_halves(half), 0.0))
    return jnp.concatenate(parts, axis=0).astype(BF16)


def merge_heads(out, rows):
    low = low_lanes(rows)
    parts = [out[g * rows : (g + 1) * rows] for g in range(4)]
    return [jnp.where(low, swap_halves(parts[2 * p]), parts[2 * p + 1]) for p in range(2)]


def kernel(
    dims,
    hist_ref,
    info_ref,
    gain1_ref,
    gain2_ref,
    wq1_hbm,
    wkv1_hbm,
    wo1_hbm,
    wq2_hbm,
    wkv2_hbm,
    wo2_hbm,
    out_ref,
    wq1,
    wkv1,
    wo1,
    wq2,
    wkv2,
    wo2,
    mid_v,
    q1buf,
    kv1buf,
    tmix,
    spread,
    sbuf1,
    rbuf1,
    q2buf,
    kvf,
    kvb,
    ibuf,
    bias_v,
    lists,
    spread2,
    sbuf2,
    rbuf2,
    w_sem,
    round_sem,
    isend,
    irecv,
    send1,
    recv1,
    ksend,
    krecv,
    send2,
    recv2,
    lsem,
):
    nt, nz, agents, nbrs = dims
    steps = nt * nz
    per_chunk = agents // CHUNKS
    crows = per_chunk * QTILES
    rows_c = per_chunk * steps
    t = lax.axis_index("tile")
    m = lax.axis_index("tm")
    z, core = m // 2, m % 2
    me = t * nz + z
    partner = (t, z * 2 + (1 - core))

    weights = [
        pltpu.make_async_copy(src, dst, w_sem.at[i])
        for i, (src, dst) in enumerate(
            (
                (wq1_hbm, wq1),
                (wkv1_hbm, wkv1),
                (wo1_hbm, wo1),
                (wq2_hbm, wq2),
                (wkv2_hbm, wkv2),
                (wo2_hbm, wo2),
            )
        )
    ]
    for copy in weights:
        copy.start()

    barrier = pltpu.get_barrier_semaphore()

    def greet_tile(r, carry):
        pl.semaphore_signal(
            barrier, inc=1, device_id=(jnp.bitwise_xor(t, r), m), device_id_type=MESH
        )
        return carry

    def greet_z(sem):
        def body(r, carry):
            pl.semaphore_signal(
                sem, inc=1, device_id=(t, lax.rem(z + r, nz) * 2 + core), device_id_type=MESH
            )
            return carry

        return body

    lax.fori_loop(1, nt, greet_tile, 0)
    lax.fori_loop(1, nz, greet_z(barrier), 0)
    pl.semaphore_signal(barrier, inc=1, device_id=partner, device_id_type=MESH)

    ibuf[t] = info_ref[...]
    kvb[0, nt] = jnp.zeros(kvb.shape[2:], BF16)
    kvb[1, nt] = jnp.zeros(kvb.shape[2:], BF16)
    bias_v[nt] = jnp.full((8, LANES), NEG, F32)

    causal = lax.broadcasted_iota(jnp.int32, (steps, steps), 0) >= lax.broadcasted_iota(
        jnp.int32, (steps, steps), 1
    )
    causal4 = jnp.concatenate([causal] * 4, axis=0)

    def temporal(h):
        first = h * rows_c
        wide = hist_ref[first : first + rows_c, :].astype(F32)
        normed = normalize(wide, gain1_ref[...])
        if h == 0:
            weights[0].wait()
        q1buf[...] = mm(normed, wq1[...])
        if h == 0:
            weights[1].wait()
        kv1buf[...] = mm(normed, wkv1[...])

        def agent(a, carry):
            rows = pl.ds(pl.multiple_of(a * steps, steps), steps)
            kv = kv1buf[rows, :]
            for k in range(KV_HEADS):
                keyval = pack_keyval(kv, k).astype(BF16)
                queries = stack_queries(q1buf[rows, k * 256 : (k + 1) * 256])
                scores = jnp.where(causal4, mm_t(queries, keyval), NEG)
                top = jnp.max(scores, axis=1, keepdims=True)
                expd = jnp.exp(scores - top)
                total = jnp.sum(expd, axis=1, keepdims=True)
                probs = (expd * (1.0 / total)).astype(BF16)
                mixed = merge_heads(mm(probs, keyval), steps)
                for p in range(2):
                    at = (2 * k + p) * LANES
                    tmix[rows, at : at + LANES] = mixed[p].astype(BF16)
            return carry

        lax.fori_loop(0, per_chunk, agent, 0)
        if h == 0:
            weights[2].wait()
        mid = hist_ref[first : first + rows_c, :].astype(F32) + mm(tmix[...], wo1[...])
        mid_v[first : first + rows_c, :] = mid.astype(BF16)
        for a in range(per_chunk):
            for q in range(QTILES):
                spread[pl.ds(q * per_chunk + a, steps, stride=crows), :] = mid[
                    a * steps : (a + 1) * steps, q * LANES : (q + 1) * LANES
                ]
        sbuf1[h] = spread[...].reshape(steps, crows, LANES).astype(BF16)
        rbuf1[h, me] = sbuf1[h, me]

    def send_chunk(h):
        def body(r, carry):
            tt = jnp.bitwise_xor(t, r // nz)
            zz = lax.rem(z + r % nz, nz)
            pltpu.make_async_remote_copy(
                src_ref=sbuf1.at[h, tt * nz + zz],
                dst_ref=rbuf1.at[h, me],
                send_sem=send1.at[h],
                recv_sem=recv1.at[h],
                device_id=(tt, zz * 2 + core),
                device_id_type=MESH,
            ).start()
            return carry

        lax.fori_loop(1, steps, body, 0)

    for h in range(CHUNKS):
        temporal(h)
        if h == 0:
            pl.semaphore_wait(barrier, nt + nz - 1)
            lax.fori_loop(1, nz, greet_z(round_sem), 0)

            def send_info(r, carry):
                pltpu.make_async_remote_copy(
                    src_ref=info_ref,
                    dst_ref=ibuf.at[t],
                    send_sem=isend,
                    recv_sem=irecv,
                    device_id=(jnp.bitwise_xor(t, r), m),
                    device_id_type=MESH,
                ).start()
                return carry

            lax.fori_loop(1, nt, send_info, 0)
            pl.semaphore_wait(round_sem, nz - 1)
        send_chunk(h)

    others = ibuf.at[pl.ds(0, nt - 1)]
    pltpu.make_async_copy(others, others, irecv).wait()
    fetch = pltpu.make_async_copy(ibuf.at[:, 8:16, :], lists, lsem)
    fetch.start()
    for i in range(nt):
        bias_v[i] = (ibuf[i, 0:8, :].astype(F32) - 1.0) * (-NEG)
    fetch.wait()

    weights[3].wait()
    weights[4].wait()
    for h in range(CHUNKS):
        landed = rbuf1.at[h, pl.ds(0, steps - 1)]
        pltpu.make_async_copy(landed, landed, recv1.at[h]).wait()
        spread[...] = rbuf1[h].astype(F32).reshape(steps * crows, LANES)
        state = jnp.concatenate(
            [
                jnp.concatenate(
                    [
                        spread[pl.ds(q * per_chunk + a, steps, stride=crows), :]
                        for q in range(QTILES)
                    ],
                    axis=1,
                )
                for a in range(per_chunk)
            ],
            axis=0,
        )
        normed = normalize(state, gain2_ref[...])
        first = h * rows_c
        q2buf[first : first + rows_c, :] = mm(normed, wq2[...])
        kv = mm(normed, wkv2[...])
        for k in range(KV_HEADS):
            kvf[k, first : first + rows_c, :] = pack_keyval(kv, k)

    def place(i, carry):
        for k in range(KV_HEADS):
            kvb[core, i, k] = jnp.concatenate(
                [
                    kvf[k, pl.ds(pl.multiple_of(a * steps + i * nz, nz), nz), :]
                    for a in range(agents)
                ],
                axis=0,
            ).astype(BF16)
        return carry

    lax.fori_loop(0, nt, place, 0)
    swap = pltpu.make_async_remote_copy(
        src_ref=kvb.at[core, pl.ds(0, nt)],
        dst_ref=kvb.at[core, pl.ds(0, nt)],
        send_sem=ksend,
        recv_sem=krecv,
        device_id=partner,
        device_id_type=MESH,
    )
    swap.start()
    swap.wait()

    arows = agents * nz
    brows = agents * QTILES
    low8 = low_lanes(8)
    per_phase = nt // PHASES

    def attend(j, phase):
        i = jnp.bitwise_xor(t, j)
        queries = jnp.concatenate(
            [
                q2buf[pl.ds(pl.multiple_of(a * steps + i * nz, nz), nz), :]
                for a in range(agents)
            ],
            axis=0,
        )
        listed = [lists[i, 0, n] for n in range(nbrs)]
        if nbrs * 2 * arows == nbrs * HEAD_DIM:
            bias = jnp.concatenate(
                [
                    jnp.where(low8, bias_v[listed[2 * p]], bias_v[listed[2 * p + 1]])
                    for p in range(nbrs // 2)
                ],
                axis=1,
            )
        else:
            bias = jnp.concatenate([bias_v[n][:, : 2 * arows] for n in listed], axis=1)
        for k in range(KV_HEADS):
            keyval = jnp.concatenate(
                [kvb[c, n, k] for n in listed for c in range(2)], axis=0
            )
            stacked = stack_queries(queries[:, k * 256 : (k + 1) * 256])
            scores = mm_t(stacked, keyval)
            nkeys = scores.shape[1]
            scores = (
                scores.reshape(4 * arows // 8, 8, nkeys) + bias[None]
            ).reshape(4 * arows, nkeys)
            top = jnp.maximum(jnp.max(scores, axis=1, keepdims=True), -1e29)
            expd = jnp.exp(scores - top)
            total = jnp.sum(expd, axis=1, keepdims=True)
            mixed = mm(expd.astype(BF16), keyval) * (1.0 / total)
            for p, block in enumerate(merge_heads(mixed, arows)):
                q = 2 * k + p
                for a in range(agents):
                    spread2[pl.ds(q * agents + a, nz, stride=brows), :] = block[
                        a * nz : (a + 1) * nz
                    ]
        sbuf2[i] = spread2[...].reshape(nz, brows, LANES).astype(BF16)

        def send(r, carry):
            zz = lax.rem(z + r, nz)
            pltpu.make_async_remote_copy(
                src_ref=sbuf2.at[i, zz],
                dst_ref=rbuf2.at[me],
                send_sem=send2,
                recv_sem=recv2.at[phase],
                device_id=(i, zz * 2 + core),
                device_id_type=MESH,
            ).start()
            return carry

        return i, send

    def own_tile():
        i, send = attend(0, 0)
        rbuf2[me] = sbuf2[t, z]
        lax.fori_loop(1, nz, send, 0)

    def other_tile(phase):
        def body(j, carry):
            i, send = attend(j, phase)
            lax.fori_loop(0, nz, send, 0)
            return carry

        return body

    own_tile()
    for phase in range(PHASES):
        lax.fori_loop(
            max(1, phase * per_phase), (phase + 1) * per_phase, other_tile(phase), 0
        )

    weights[5].wait()
    psteps = per_phase * nz
    for phase in range(PHASES):
        count = psteps - (1 if phase == 0 else 0)
        landed = rbuf2.at[pl.ds(0, count)]
        pltpu.make_async_copy(landed, landed, recv2.at[phase]).wait()
        group = jnp.bitwise_xor(t // per_phase, phase)
        at = pl.multiple_of(group * psteps, psteps)
        back = rbuf2[pl.ds(at, psteps)].astype(F32).reshape(psteps * brows, LANES)
        spread[pl.ds(0, psteps * brows), :] = back
        mixed = jnp.concatenate(
            [
                jnp.concatenate(
                    [
                        spread[pl.ds(q * agents + a, psteps, stride=brows), :]
                        for q in range(QTILES)
                    ],
                    axis=1,
                )
                for a in range(agents)
            ],
            axis=0,
        ).astype(BF16)
        projected = mm(mixed, wo2[...])
        for a in range(agents):
            here = pl.ds(pl.multiple_of(a * steps + at, psteps), psteps)
            out_ref[here, :] = (
                mid_v[here, :].astype(F32) + projected[a * psteps : (a + 1) * psteps]
            ).astype(BF16)

    pltpu.make_async_copy(others, others, isend).wait()
    for h in range(CHUNKS):
        gone = sbuf1.at[h, pl.ds(0, steps - 1)]
        pltpu.make_async_copy(gone, gone, send1.at[h]).wait()
    gone = rbuf2.at[pl.ds(0, steps - 1)]
    pltpu.make_async_copy(gone, gone, send2).wait()


def per_device(
    nt,
    nz,
    histories,
    gain_time,
    wq_time,
    wkv_time,
    wo_time,
    gain_space,
    wq_space,
    wkv_space,
    wo_space,
    neighbours,
    nbr_valid,
    agent_valid,
):
    _, agents, steps, _ = histories.shape
    nbrs = neighbours.shape[1]
    half = agents * nz
    alive = agent_valid.reshape(nz, 2, agents).transpose(1, 2, 0).reshape(1, 2 * half)
    alive = jnp.tile(alive, (8, LANES // (2 * half)))
    listed = jnp.where(nbr_valid > 0, neighbours, nt)
    listed = jnp.tile(jnp.pad(listed, ((0, 0), (0, LANES - nbrs))), (8, 1))
    info = jnp.concatenate([alive, listed], axis=0)

    crows = agents // CHUNKS * QTILES
    brows = agents * QTILES
    rows_c = agents // CHUNKS * steps
    vmem = pl.BlockSpec(memory_space=pltpu.VMEM)
    hbm = pl.BlockSpec(memory_space=pl.ANY)
    out = pl.pallas_call(
        functools.partial(kernel, (nt, nz, agents, nbrs)),
        out_shape=jax.ShapeDtypeStruct((agents * steps, D), BF16),
        in_specs=[vmem] * 4 + [hbm] * 6,
        out_specs=vmem,
        scratch_shapes=[
            pltpu.VMEM((D, D), BF16),
            pltpu.VMEM((D, 512), BF16),
            pltpu.VMEM((D, D), BF16),
            pltpu.VMEM((D, D), BF16),
            pltpu.VMEM((D, 512), BF16),
            pltpu.VMEM((D, D), BF16),
            pltpu.VMEM((agents * steps, D), BF16),
            pltpu.VMEM((rows_c, D), F32),
            pltpu.VMEM((rows_c, 512), F32),
            pltpu.VMEM((rows_c, D), BF16),
            pltpu.VMEM((steps * crows, LANES), F32),
            pltpu.VMEM((CHUNKS, steps, crows, LANES), BF16),
            pltpu.VMEM((CHUNKS, steps, crows, LANES), BF16),
            pltpu.VMEM((agents * steps, D), F32),
            pltpu.VMEM((KV_HEADS, agents * steps, LANES), F32),
            pltpu.VMEM((2, nt + 1, KV_HEADS, half, LANES), BF16),
            pltpu.VMEM((nt, 16, LANES), jnp.int32),
            pltpu.VMEM((nt + 1, 8, LANES), F32),
            pltpu.SMEM((nt, 8, LANES), jnp.int32),
            pltpu.VMEM((nz * brows, LANES), F32),
            pltpu.VMEM((nt, nz, brows, LANES), BF16),
            pltpu.VMEM((steps, brows, LANES), BF16),
            pltpu.SemaphoreType.DMA((6,)),
            pltpu.SemaphoreType.REGULAR,
            pltpu.SemaphoreType.DMA,
            pltpu.SemaphoreType.DMA,
            pltpu.SemaphoreType.DMA((CHUNKS,)),
            pltpu.SemaphoreType.DMA((CHUNKS,)),
            pltpu.SemaphoreType.DMA,
            pltpu.SemaphoreType.DMA,
            pltpu.SemaphoreType.DMA,
            pltpu.SemaphoreType.DMA((PHASES,)),
            pltpu.SemaphoreType.DMA,
        ],
        compiler_params=pltpu.CompilerParams(
            collective_id=0, has_side_effects=True, vmem_limit_bytes=60 * 1024 * 1024
        ),
    )(
        histories.reshape(agents * steps, D),
        info,
        gain_time.reshape(1, D),
        gain_space.reshape(1, D),
        wq_time,
        wkv_time,
        wo_time,
        wq_space,
        wkv_space,
        wo_space,
    )
    return out.reshape(1, agents, steps, D)


def solution(mesh):
    return jax.shard_map(
        functools.partial(per_device, mesh.shape["tile"], mesh.shape["tm"] // 2),
        mesh=mesh,
        in_specs=(
            P("tile", "tm", None, None),
            P(),
            P(),
            P(),
            P(),
            P(),
            P(),
            P(),
            P(),
            P("tile", None),
            P("tile", None),
            P("tile", None),
        ),
        out_specs=P("tile", "tm", None, None),
        check_vma=False,
    )
```

```python
import contextlib
import functools

import jax
import jax.numpy as jnp
from jax import lax
from jax.experimental import pallas as pl
from jax.experimental.pallas import tpu as pltpu
from jax.sharding import PartitionSpec as P

HEADS = 16
KV_HEADS = 4
HEAD_DIM = 64
D = 1024
LANES = 128
QTILES = D // LANES
MESH = pl.DeviceIdType.MESH
BF16 = jnp.bfloat16
F32 = jnp.float32
PHASES = 4
NEG = -1e30


def scope(name):
    return contextlib.nullcontext()


def normalize(wide, gain):
    meansq = jnp.mean(wide * wide, axis=-1, keepdims=True)
    return (wide * lax.rsqrt(meansq + 1e-05) * gain).astype(BF16)


def mm(a, b):
    return jnp.dot(a, b, preferred_element_type=F32)


def mm_t(a, b):
    return lax.dot_general(a, b, (((1,), (1,)), ((), ())), preferred_element_type=F32)


def low_lanes(rows):
    return lax.broadcasted_iota(jnp.int32, (rows, LANES), 1) < HEAD_DIM


def swap_halves(x):
    return pltpu.roll(x, HEAD_DIM, 1)


def pack_keyval(kv, k):
    at = (k // 2) * LANES
    keys = kv[:, at : at + LANES]
    values = kv[:, 2 * LANES + at : 3 * LANES + at]
    low = low_lanes(kv.shape[0])
    if k % 2 == 0:
        return jnp.where(low, keys, swap_halves(values))
    return jnp.where(low, swap_halves(keys), values)


def stack_queries(block, rest):
    low = low_lanes(block.shape[0])
    parts = []
    for pair in range(2):
        half = block[:, pair * LANES : (pair + 1) * LANES] * 0.125
        parts.append(jnp.where(low, half, rest))
        parts.append(jnp.where(low, swap_halves(half), rest))
    return jnp.concatenate(parts, axis=0).astype(BF16)


def merge_heads(out, rows):
    low = low_lanes(rows)
    parts = [out[g * rows : (g + 1) * rows] for g in range(4)]
    return [jnp.where(low, swap_halves(parts[2 * p]), parts[2 * p + 1]) for p in range(2)]


def kernel(
    dims,
    hist_hbm,
    gain1_ref,
    gain2_ref,
    neigh_ref,
    valid_ref,
    alive_ref,
    wq1_hbm,
    wkv1_hbm,
    wo1_hbm,
    wq2_hbm,
    wkv2_hbm,
    wo2_hbm,
    out_hbm,
    hist_v,
    wq1,
    wkv1,
    wo1,
    wq2,
    wkv2,
    wo2,
    mid_v,
    q1buf,
    tmix,
    spread,
    sbuf1,
    rbuf1,
    q2buf,
    kvf,
    kvb,
    keys_v,
    values_v,
    bias_v,
    nbuf,
    vbuf,
    abuf,
    nlist,
    vlist,
    spread2,
    sbuf2,
    rbuf2,
    w_sem,
    h_sem,
    isend,
    irecv,
    own_sem,
    send1,
    recv1,
    ksend,
    krecv,
    send2,
    recv2,
    lsem,
    out_v,
    out_sem,
):
    nt, nz, agents, nbrs = dims
    steps = nt * nz
    half = agents // 2 * nz
    t = lax.axis_index("tile")
    m = lax.axis_index("tm")
    z, core = m // 2, m % 2
    me = t * nz + z
    partner = (t, z * 2 + (1 - core))

    def history(a):
        rows = pl.ds(a * steps, steps)
        return pltpu.make_async_copy(hist_hbm.at[rows], hist_v.at[rows], h_sem.at[a])

    def weight(i):
        src, dst = (
            (wq1_hbm, wq1),
            (wkv1_hbm, wkv1),
            (wo1_hbm, wo1),
            (wq2_hbm, wq2),
            (wkv2_hbm, wkv2),
            (wo2_hbm, wo2),
        )[i]
        return pltpu.make_async_copy(src, dst, w_sem.at[i])

    history(0).start()
    weight(1).start()
    weight(0).start()

    barrier = pltpu.get_barrier_semaphore()

    spots = []
    for r in range(nz):
        k = (r + 1) // 2
        dz = (nz // 2 - k if r % 2 == 1 else nz // 2 + k) % nz
        zz = jnp.bitwise_and(z + dz, nz - 1)
        spots.append((zz, zz * 2 + core))

    def far_four(n):
        return jnp.where(n == 0, 2, jnp.where(n == 3, 0, 2 * n - 1))

    def far_tile(n):
        if nt != 16:
            return far_four(n)
        high = jnp.where(n < 4, 2, jnp.where(n < 8, 1, jnp.where(n < 12, 3, 0)))
        return high * 4 + far_four(jnp.bitwise_and(n, 3))

    def each_peer(act):
        def body(n, carry):
            tt = jnp.bitwise_xor(t, far_tile(n))
            for zz, tm in spots:
                act(tt, zz, tm)
            return carry

        lax.fori_loop(0, nt - 1, body, 0)
        for zz, tm in spots[:-1]:
            act(t, zz, tm)

    each_peer(
        lambda tt, zz, tm: pl.semaphore_signal(
            barrier, inc=1, device_id=(tt, tm), device_id_type=MESH
        )
    )
    pl.semaphore_signal(barrier, inc=1, device_id=partner, device_id_type=MESH)

    weight(2).start()
    for a in range(1, agents):
        history(a).start()

    own = [
        pltpu.make_async_copy(src, dst.at[t], own_sem.at[i])
        for i, (src, dst) in enumerate(
            ((neigh_ref, nbuf), (valid_ref, vbuf), (alive_ref, abuf))
        )
    ]

    causal = lax.broadcasted_iota(jnp.int32, (steps, steps), 0) >= lax.broadcasted_iota(
        jnp.int32, (steps, steps), 1
    )
    causal4 = jnp.concatenate([causal] * 4, axis=0)

    def temporal(h):
        rows = pl.ds(h * steps, steps)
        with scope(f"HISTW{h}"):
            history(h).wait()
        normed = normalize(hist_v[rows, :].astype(F32), gain1_ref[...])
        if h == 0:
            with scope("W1"):
                weight(1).wait()
        kv = mm(normed, wkv1[...])
        if h == 0:
            with scope("W0"):
                weight(0).wait()
        q1buf[...] = mm(normed, wq1[...])
        if h == 0:
            for i in range(3, 6):
                weight(i).start()
        for k in range(KV_HEADS):
            keyval = pack_keyval(kv, k).astype(BF16)
            queries = stack_queries(q1buf[:, k * 256 : (k + 1) * 256], 0.0)
            scores = jnp.where(causal4, mm_t(queries, keyval), NEG)
            top = jnp.max(scores, axis=1, keepdims=True)
            expd = jnp.exp(scores - top)
            total = jnp.sum(expd, axis=1, keepdims=True)
            probs = (expd * (1.0 / total)).astype(BF16)
            mixed = merge_heads(mm(probs, keyval), steps)
            for p in range(2):
                at = (2 * k + p) * LANES
                tmix[:, at : at + LANES] = mixed[p].astype(BF16)
        if h == 0:
            with scope("W2"):
                weight(2).wait()
        mid = hist_v[rows, :].astype(F32) + mm(tmix[...], wo1[...])
        mid_v[rows, :] = mid.astype(BF16)
        for q in range(QTILES):
            spread[pl.ds(q, steps, stride=QTILES), :] = mid[:, q * LANES : (q + 1) * LANES]
        sbuf1[h] = spread[pl.ds(0, steps * QTILES), :].reshape(steps, QTILES, LANES).astype(BF16)
        rbuf1[h, me] = sbuf1[h, me]

    def send_chunk(h):
        each_peer(
            lambda tt, zz, tm: pltpu.make_async_remote_copy(
                src_ref=sbuf1.at[h, tt * nz + zz],
                dst_ref=rbuf1.at[h, me],
                send_sem=send1.at[h],
                recv_sem=recv1.at[h],
                device_id=(tt, tm),
                device_id_type=MESH,
            ).start()
        )

    for h in range(agents):
        with scope(f"TEMP{h}"):
            temporal(h)
        if h == 0:
            with scope("BARR"):
                pl.semaphore_wait(barrier, steps)
        with scope(f"SEND{h}"):
            send_chunk(h)

    for copy in own:
        copy.start()

    def send_lists(r, carry):
        for i, (src, dst) in enumerate(
            ((neigh_ref, nbuf), (valid_ref, vbuf), (alive_ref, abuf))
        ):
            pltpu.make_async_remote_copy(
                src_ref=src,
                dst_ref=dst.at[t],
                send_sem=isend.at[i],
                recv_sem=irecv.at[i],
                device_id=(jnp.bitwise_xor(t, r), m),
                device_id_type=MESH,
            ).start()
        return carry

    lax.fori_loop(1, nt, send_lists, 0)
    nkeys = 2 * agents * nz
    keys_v[nt] = jnp.where(
        lax.broadcasted_iota(jnp.int32, (nkeys, LANES), 1) == HEAD_DIM, NEG, 0.0
    ).astype(BF16)[None].reshape(1, 4, nkeys // 4, LANES) + jnp.zeros(keys_v.shape[1:], BF16)
    values_v[nt] = jnp.zeros(values_v.shape[1:], BF16)
    with scope("IWAIT"):
        for copy in own:
            copy.wait()
        for i, dst in enumerate((nbuf, vbuf, abuf)):
            others = dst.at[pl.ds(0, nt - 1)]
            pltpu.make_async_copy(others, others, irecv.at[i]).wait()
    fetch = [
        pltpu.make_async_copy(nbuf, nlist, lsem.at[0]),
        pltpu.make_async_copy(vbuf, vlist, lsem.at[1]),
    ]
    for copy in fetch:
        copy.start()
    key = lax.broadcasted_iota(jnp.int32, (nkeys, nkeys), 0)
    who = ((key % nz) * 2 + key // (nkeys // 2)) * agents + (key // nz) % agents
    order = (who == lax.broadcasted_iota(jnp.int32, (nkeys, nkeys), 1)).astype(F32).astype(BF16)
    lane_row = lax.broadcasted_iota(jnp.int32, (LANES, nkeys), 0) == HEAD_DIM
    unit = (lax.broadcasted_iota(jnp.int32, (nkeys, LANES), 1) == HEAD_DIM).astype(F32)
    for i in range(nt):
        row = jnp.where(lane_row, abuf[i].astype(F32), 0.0).astype(BF16)
        bias_v[i] = ((mm_t(order, row) - unit) * (-NEG)).astype(BF16).reshape(bias_v.shape[1:])

    weight(3).wait()
    weight(4).wait()

    def unpack(side, part):
        low = low_lanes(half)

        def body(i, carry):
            for k in range(KV_HEADS):
                both = kvb[side, part, i, k].astype(F32)
                at = 2 * side + part
                keys_v[i, k, at] = jnp.where(low, both, bias_v[i, at].astype(F32)).astype(BF16)
                values_v[i, k, at] = jnp.where(low, 1.0, both).astype(BF16)
            return carry

        lax.fori_loop(0, nt, body, 0)

    def swap(part):
        return pltpu.make_async_remote_copy(
            src_ref=kvb.at[core, part],
            dst_ref=kvb.at[core, part],
            send_sem=ksend.at[part],
            recv_sem=krecv.at[part],
            device_id=partner,
            device_id_type=MESH,
        )

    for h in range(agents):
        landed = rbuf1.at[h, pl.ds(0, steps - 1)]
        with scope(f"RWAIT{h}"):
            pltpu.make_async_copy(landed, landed, recv1.at[h]).wait()
        spread[pl.ds(0, steps * QTILES), :] = rbuf1[h].astype(F32).reshape(steps * QTILES, LANES)
        state = jnp.concatenate(
            [spread[pl.ds(q, steps, stride=QTILES), :] for q in range(QTILES)], axis=1
        )
        normed = normalize(state, gain2_ref[...])
        rows = pl.ds(h * steps, steps)
        kv = mm(normed, wkv2[...])
        for k in range(KV_HEADS):
            kvf[k, rows, :] = pack_keyval(kv, k)
        if h % 2 == 1:
            part = h // 2

            def place(i, carry):
                for k in range(KV_HEADS):
                    kvb[core, part, i, k] = jnp.concatenate(
                        [
                            kvf[k, pl.ds(pl.multiple_of(a * steps + i * nz, nz), nz), :]
                            for a in (h - 1, h)
                        ],
                        axis=0,
                    ).astype(BF16)
                return carry

            lax.fori_loop(0, nt, place, 0)
            swap(part).start()
        q2buf[rows, :] = mm(normed, wq2[...])
        if h % 2 == 1:
            unpack(core, part)
    for part in range(2):
        with scope(f"SWAP{part}"):
            swap(part).wait()
        with scope("UNP"):
            unpack(1 - core, part)
    with scope("FETCH"):
        for copy in fetch:
            copy.wait()

    arows = agents * nz
    brows = agents * QTILES
    per_phase = nt // PHASES
    unit_a = (lax.broadcasted_iota(jnp.int32, (arows, LANES), 1) == HEAD_DIM).astype(F32)
    low_a = low_lanes(arows)

    def attend(j, phase):
        i = jnp.bitwise_xor(t, j)
        queries = jnp.concatenate(
            [
                q2buf[pl.ds(pl.multiple_of(a * steps + i * nz, nz), nz), :]
                for a in range(agents)
            ],
            axis=0,
        )
        listed = [
            jnp.where(vlist[i, 0, n] > 0, nlist[i, 0, n], nt) for n in range(nbrs)
        ]
        def score(k):
            keys = jnp.concatenate([keys_v[n, k].reshape(nkeys, LANES) for n in listed], axis=0)
            return mm_t(stack_queries(queries[:, k * 256 : (k + 1) * 256], unit_a), keys)

        ahead = score(0)
        for k in range(KV_HEADS):
            scores = ahead
            if k + 1 < KV_HEADS:
                ahead = score(k + 1)
            values = jnp.concatenate(
                [values_v[n, k].reshape(nkeys, LANES) for n in listed], axis=0
            )
            top = jnp.maximum(jnp.max(scores, axis=1, keepdims=True), -1e29)
            mixed = mm(jnp.exp(scores - top).astype(BF16), values)
            for p in range(2):
                even = mixed[2 * p * arows : (2 * p + 1) * arows]
                odd = mixed[(2 * p + 1) * arows : (2 * p + 2) * arows]
                swapped_even, swapped_odd = swap_halves(even), swap_halves(odd)
                block = jnp.where(low_a, swapped_even, odd) * (
                    1.0 / jnp.where(low_a, even, swapped_odd)
                )
                q = 2 * k + p
                for a in range(agents):
                    spread2[pl.ds(q * agents + a, nz, stride=brows), :] = block[
                        a * nz : (a + 1) * nz
                    ]
        sbuf2[i] = spread2[...].reshape(nz, brows, LANES).astype(BF16)

        for zz, tm in spots if phase is not None else spots[:-1]:
            pltpu.make_async_remote_copy(
                src_ref=sbuf2.at[i, zz],
                dst_ref=rbuf2.at[me],
                send_sem=send2,
                recv_sem=recv2.at[PHASES - 1 if phase is None else phase],
                device_id=(i, tm),
                device_id_type=MESH,
            ).start()

    def other_tile(phase):
        def body(n, carry):
            attend(far_tile(n), phase)
            return carry

        return body

    for phase in range(PHASES):
        with scope(f"ATT{phase}"):
            lax.fori_loop(
                phase * per_phase, min((phase + 1) * per_phase, nt - 1), other_tile(phase), 0
            )
    with scope("OWN"):
        attend(0, None)
        rbuf2[me] = sbuf2[t, z]

    weight(5).wait()
    psteps = per_phase * nz
    results = []
    for phase in range(PHASES):
        count = psteps - (1 if phase == PHASES - 1 else 0)
        landed = rbuf2.at[pl.ds(0, count)]
        with scope(f"HWAIT{phase}"):
            pltpu.make_async_copy(landed, landed, recv2.at[phase]).wait()
        group = jnp.bitwise_xor(t // per_phase, (2, 1, 3, 0)[phase])
        at = pl.multiple_of(group * psteps, psteps)
        back = rbuf2[pl.ds(at, psteps)].astype(F32).reshape(psteps * brows, LANES)
        spread[pl.ds(0, psteps * brows), :] = back
        mixed = jnp.concatenate(
            [
                jnp.concatenate(
                    [
                        spread[pl.ds(q * agents + a, psteps, stride=brows), :]
                        for q in range(QTILES)
                    ],
                    axis=1,
                )
                for a in range(agents)
            ],
            axis=0,
        ).astype(BF16)
        projected = mm(mixed, wo2[...])
        for a in range(agents):
            here = pl.ds(pl.multiple_of(a * steps + at, psteps), psteps)
            out_v[here, :] = (
                mid_v[here, :].astype(F32) + projected[a * psteps : (a + 1) * psteps]
            ).astype(BF16)
            result = pltpu.make_async_copy(
                out_v.at[here], out_hbm.at[here], out_sem.at[phase * agents + a]
            )
            result.start()
            results.append(result)

    with scope("FIN"):
        for result in results:
            result.wait()
    for i, dst in enumerate((nbuf, vbuf, abuf)):
        others = dst.at[pl.ds(0, nt - 1)]
        pltpu.make_async_copy(others, others, isend.at[i]).wait()
    for h in range(agents):
        gone = sbuf1.at[h, pl.ds(0, steps - 1)]
        pltpu.make_async_copy(gone, gone, send1.at[h]).wait()
    gone = rbuf2.at[pl.ds(0, steps - 1)]
    pltpu.make_async_copy(gone, gone, send2).wait()


def per_device(
    nt,
    nz,
    histories,
    gain_time,
    wq_time,
    wkv_time,
    wo_time,
    gain_space,
    wq_space,
    wkv_space,
    wo_space,
    neighbours,
    nbr_valid,
    agent_valid,
):
    _, agents, steps, _ = histories.shape
    nbrs = neighbours.shape[1]
    half = agents // 2 * nz
    brows = agents * QTILES
    vmem = pl.BlockSpec(memory_space=pltpu.VMEM)
    hbm = pl.BlockSpec(memory_space=pl.ANY)
    dma = pltpu.SemaphoreType.DMA
    out = pl.pallas_call(
        functools.partial(kernel, (nt, nz, agents, nbrs)),
        out_shape=jax.ShapeDtypeStruct((agents * steps, D), BF16),
        in_specs=[hbm, vmem, vmem] + [hbm] * 9,
        out_specs=hbm,
        scratch_shapes=[
            pltpu.VMEM((agents * steps, D), BF16),
            pltpu.VMEM((D, D), BF16),
            pltpu.VMEM((D, 512), BF16),
            pltpu.VMEM((D, D), BF16),
            pltpu.VMEM((D, D), BF16),
            pltpu.VMEM((D, 512), BF16),
            pltpu.VMEM((D, D), BF16),
            pltpu.VMEM((agents * steps, D), BF16),
            pltpu.VMEM((steps, D), F32),
            pltpu.VMEM((steps, D), BF16),
            pltpu.VMEM((max(steps * QTILES, nt // PHASES * nz * brows), LANES), F32),
            pltpu.VMEM((agents, steps, QTILES, LANES), BF16),
            pltpu.VMEM((agents, steps, QTILES, LANES), BF16),
            pltpu.VMEM((agents * steps, D), F32),
            pltpu.VMEM((KV_HEADS, agents * steps, LANES), F32),
            pltpu.VMEM((2, 2, nt, KV_HEADS, half, LANES), BF16),
            pltpu.VMEM((nt + 1, KV_HEADS, 4, half, LANES), BF16),
            pltpu.VMEM((nt + 1, KV_HEADS, 4, half, LANES), BF16),
            pltpu.VMEM((nt, 4, half, LANES), BF16),
            pltpu.VMEM((nt, 1, nbrs), jnp.int32),
            pltpu.VMEM((nt, 1, nbrs), jnp.int32),
            pltpu.VMEM((nt, 1, 4 * half), jnp.int32),
            pltpu.SMEM((nt, 1, nbrs), jnp.int32),
            pltpu.SMEM((nt, 1, nbrs), jnp.int32),
            pltpu.VMEM((nz * brows, LANES), F32),
            pltpu.VMEM((nt, nz, brows, LANES), BF16),
            pltpu.VMEM((steps, brows, LANES), BF16),
            dma((6,)),
            dma((agents,)),
            dma((3,)),
            dma((3,)),
            dma((3,)),
            dma((agents,)),
            dma((agents,)),
            dma((2,)),
            dma((2,)),
            dma,
            dma((PHASES,)),
            dma((2,)),
            pltpu.VMEM((agents * steps, D), BF16),
            dma((PHASES * agents,)),
        ],
        compiler_params=pltpu.CompilerParams(
            collective_id=0, has_side_effects=True, vmem_limit_bytes=60 * 1024 * 1024
        ),
    )(
        histories.reshape(agents * steps, D),
        gain_time.reshape(1, D),
        gain_space.reshape(1, D),
        neighbours,
        nbr_valid,
        agent_valid,
        wq_time,
        wkv_time,
        wo_time,
        wq_space,
        wkv_space,
        wo_space,
    )
    return out.reshape(1, agents, steps, D)


def solution(mesh):
    return jax.shard_map(
        functools.partial(per_device, mesh.shape["tile"], mesh.shape["tm"] // 2),
        mesh=mesh,
        in_specs=(
            P("tile", "tm", None, None),
            P(),
            P(),
            P(),
            P(),
            P(),
            P(),
            P(),
            P(),
            P("tile", None),
            P("tile", None),
            P("tile", None),
        ),
        out_specs=P("tile", "tm", None, None),
        check_vma=False,
    )
```

```python
import contextlib
import functools

import jax
import jax.numpy as jnp
from jax import lax
from jax.experimental import pallas as pl
from jax.experimental.pallas import tpu as pltpu
from jax.sharding import PartitionSpec as P

HEADS = 16
KV_HEADS = 4
HEAD_DIM = 64
D = 1024
LANES = 128
QTILES = D // LANES
MESH = pl.DeviceIdType.MESH
BF16 = jnp.bfloat16
F32 = jnp.float32
PHASES = 4
NEG = -1e30


def scope(name):
    return contextlib.nullcontext()


def normalize(wide, gain):
    meansq = jnp.mean(wide * wide, axis=-1, keepdims=True)
    return (wide * lax.rsqrt(meansq + 1e-05) * gain).astype(BF16)


def mm(a, b):
    return jnp.dot(a, b, preferred_element_type=F32)


def mm_t(a, b):
    return lax.dot_general(a, b, (((1,), (1,)), ((), ())), preferred_element_type=F32)


def low_lanes(rows):
    return lax.broadcasted_iota(jnp.int32, (rows, LANES), 1) < HEAD_DIM


def swap_halves(x):
    return pltpu.roll(x, HEAD_DIM, 1)


def pack_keyval(kv, k):
    at = (k // 2) * LANES
    keys = kv[:, at : at + LANES]
    values = kv[:, 2 * LANES + at : 3 * LANES + at]
    low = low_lanes(kv.shape[0])
    if k % 2 == 0:
        return jnp.where(low, keys, swap_halves(values))
    return jnp.where(low, swap_halves(keys), values)


def stack_queries(block, rest):
    low = low_lanes(block.shape[0])
    parts = []
    for pair in range(2):
        half = block[:, pair * LANES : (pair + 1) * LANES] * 0.125
        parts.append(jnp.where(low, half, rest))
        parts.append(jnp.where(low, swap_halves(half), rest))
    return jnp.concatenate(parts, axis=0).astype(BF16)


def merge_heads(out, rows):
    low = low_lanes(rows)
    parts = [out[g * rows : (g + 1) * rows] for g in range(4)]
    return [jnp.where(low, swap_halves(parts[2 * p]), parts[2 * p + 1]) for p in range(2)]


def kernel(
    dims,
    hist_hbm,
    gain1_ref,
    gain2_ref,
    neigh_ref,
    valid_ref,
    alive_ref,
    wq1_hbm,
    wkv1_hbm,
    wo1_hbm,
    wq2_hbm,
    wkv2_hbm,
    wo2_hbm,
    out_hbm,
    hist_v,
    wq1,
    wkv1,
    wo1,
    wq2,
    wkv2,
    wo2,
    mid_v,
    q1buf,
    tmix,
    spread,
    sbuf1,
    rbuf1,
    q2buf,
    kvf,
    kvb,
    keys_v,
    values_v,
    bias_v,
    nbuf,
    vbuf,
    abuf,
    nlist,
    vlist,
    spread2,
    sbuf2,
    rbuf2,
    w_sem,
    h_sem,
    isend,
    irecv,
    own_sem,
    send1,
    recv1,
    ksend,
    krecv,
    send2,
    recv2,
    lsem,
    out_v,
    out_sem,
):
    nt, nz, agents, nbrs = dims
    steps = nt * nz
    half = agents // 2 * nz
    t = lax.axis_index("tile")
    m = lax.axis_index("tm")
    z, core = m // 2, m % 2
    me = t * nz + z
    partner = (t, z * 2 + (1 - core))

    def history(a):
        rows = pl.ds(a * steps, steps)
        return pltpu.make_async_copy(hist_hbm.at[rows], hist_v.at[rows], h_sem.at[a])

    def weight(i):
        src, dst = (
            (wq1_hbm, wq1),
            (wkv1_hbm, wkv1),
            (wo1_hbm, wo1),
            (wq2_hbm, wq2),
            (wkv2_hbm, wkv2),
            (wo2_hbm, wo2),
        )[i]
        return pltpu.make_async_copy(src, dst, w_sem.at[i])

    history(0).start()
    weight(1).start()
    weight(0).start()

    barrier = pltpu.get_barrier_semaphore()

    spots = []
    for r in range(nz):
        k = (r + 1) // 2
        dz = (nz // 2 - k if r % 2 == 1 else nz // 2 + k) % nz
        zz = jnp.bitwise_and(z + dz, nz - 1)
        spots.append((zz, zz * 2 + core))

    def far_four(n):
        return jnp.where(n == 0, 2, jnp.where(n == 3, 0, 2 * n - 1))

    def far_tile(n):
        if nt != 16:
            return far_four(n)
        high = jnp.where(n < 4, 2, jnp.where(n < 8, 1, jnp.where(n < 12, 3, 0)))
        return high * 4 + far_four(jnp.bitwise_and(n, 3))

    def each_peer(act):
        def body(n, carry):
            tt = jnp.bitwise_xor(t, far_tile(n))
            for zz, tm in spots:
                act(tt, zz, tm)
            return carry

        lax.fori_loop(0, nt - 1, body, 0)
        for zz, tm in spots[:-1]:
            act(t, zz, tm)

    parity = jnp.bitwise_and(jnp.bitwise_xor(jnp.bitwise_xor(t, t // 4), z), 1)
    evens = (10, 2, 8, 5, 7, 13, 15, 0) if nt == 16 else (2, 0)

    def each_of_group(group, act):
        flip = parity if group == 0 else 1 - parity
        places = [[], []]
        for r in range(nz // 2):
            k = (r + 1) // 2
            away = (nz // 4 - k if r % 2 == 1 else nz // 4 + k) * 2 % nz
            for side, shift in enumerate((flip, 1 - flip)):
                zz = jnp.bitwise_and(z + shift + away, nz - 1)
                places[side].append((zz, zz * 2 + core))

        def body(n, carry):
            j = 0
            for at, even in enumerate(evens[:-1]):
                j = jnp.where(n == at, even, j)
            tt = jnp.bitwise_xor(t, j)
            for zz, tm in places[0]:
                act(tt, zz, tm)
            tt = jnp.bitwise_xor(tt, 1)
            for zz, tm in places[1]:
                act(tt, zz, tm)
            return carry

        lax.fori_loop(0, len(evens) - 1, body, 0)
        for zz, tm in places[1]:
            act(jnp.bitwise_xor(t, 1), zz, tm)
        for zz, tm in places[0][:-1]:
            act(t, zz, tm)

        @pl.when(flip == 1)
        def _():
            act(t, *places[0][-1])

    each_peer(
        lambda tt, zz, tm: pl.semaphore_signal(
            barrier, inc=1, device_id=(tt, tm), device_id_type=MESH
        )
    )
    pl.semaphore_signal(barrier, inc=1, device_id=partner, device_id_type=MESH)

    weight(2).start()
    for a in range(1, agents):
        history(a).start()

    own = [
        pltpu.make_async_copy(src, dst.at[t], own_sem.at[i])
        for i, (src, dst) in enumerate(
            ((neigh_ref, nbuf), (valid_ref, vbuf), (alive_ref, abuf))
        )
    ]

    causal = lax.broadcasted_iota(jnp.int32, (steps, steps), 0) >= lax.broadcasted_iota(
        jnp.int32, (steps, steps), 1
    )
    causal4 = jnp.concatenate([causal] * 4, axis=0)

    def temporal(h):
        rows = pl.ds(h * steps, steps)
        with scope(f"HISTW{h}"):
            history(h).wait()
        normed = normalize(hist_v[rows, :].astype(F32), gain1_ref[...])
        if h == 0:
            with scope("W1"):
                weight(1).wait()
        kv = mm(normed, wkv1[...])
        if h == 0:
            with scope("W0"):
                weight(0).wait()
        q1buf[...] = mm(normed, wq1[...])
        if h == 0:
            for i in range(3, 6):
                weight(i).start()
        for k in range(KV_HEADS):
            keyval = pack_keyval(kv, k).astype(BF16)
            queries = stack_queries(q1buf[:, k * 256 : (k + 1) * 256], 0.0)
            scores = jnp.where(causal4, mm_t(queries, keyval), NEG)
            top = jnp.max(scores, axis=1, keepdims=True)
            expd = jnp.exp(scores - top)
            total = jnp.sum(expd, axis=1, keepdims=True)
            probs = (expd * (1.0 / total)).astype(BF16)
            mixed = merge_heads(mm(probs, keyval), steps)
            for p in range(2):
                at = (2 * k + p) * LANES
                tmix[:, at : at + LANES] = mixed[p].astype(BF16)
        if h == 0:
            with scope("W2"):
                weight(2).wait()
        mid = hist_v[rows, :].astype(F32) + mm(tmix[...], wo1[...])
        mid_v[rows, :] = mid.astype(BF16)
        for q in range(QTILES):
            spread[pl.ds(q, steps, stride=QTILES), :] = mid[:, q * LANES : (q + 1) * LANES]
        sbuf1[h] = spread[pl.ds(0, steps * QTILES), :].reshape(steps, QTILES, LANES).astype(BF16)
        rbuf1[h, me] = sbuf1[h, me]

    def send_chunk(h, group):
        each_of_group(
            group,
            lambda tt, zz, tm: pltpu.make_async_remote_copy(
                src_ref=sbuf1.at[h, tt * nz + zz],
                dst_ref=rbuf1.at[h, me],
                send_sem=send1.at[h],
                recv_sem=recv1.at[h],
                device_id=(tt, tm),
                device_id_type=MESH,
            ).start(),
        )

    def send_lists(r, carry):
        for i, (src, dst) in enumerate(
            ((neigh_ref, nbuf), (valid_ref, vbuf), (alive_ref, abuf))
        ):
            pltpu.make_async_remote_copy(
                src_ref=src,
                dst_ref=dst.at[t],
                send_sem=isend.at[i],
                recv_sem=irecv.at[i],
                device_id=(jnp.bitwise_xor(t, r), m),
                device_id_type=MESH,
            ).start()
        return carry

    for h in range(agents):
        with scope(f"TEMP{h}"):
            temporal(h)
        if h == 0:
            with scope("BARR"):
                pl.semaphore_wait(barrier, steps)
        with scope(f"SEND{h}"):
            send_chunk(h, 0)
            if h == 0:
                for copy in own:
                    copy.start()
                lax.fori_loop(1, nt, send_lists, 0)
    with scope("SENDB"):
        for h in range(agents):
            send_chunk(h, 1)

    nkeys = 2 * agents * nz
    keys_v[nt] = jnp.where(
        lax.broadcasted_iota(jnp.int32, (nkeys, LANES), 1) == HEAD_DIM, NEG, 0.0
    ).astype(BF16)[None].reshape(1, 4, nkeys // 4, LANES) + jnp.zeros(keys_v.shape[1:], BF16)
    values_v[nt] = jnp.zeros(values_v.shape[1:], BF16)
    with scope("IWAIT"):
        for copy in own:
            copy.wait()
        for i, dst in enumerate((nbuf, vbuf, abuf)):
            others = dst.at[pl.ds(0, nt - 1)]
            pltpu.make_async_copy(others, others, irecv.at[i]).wait()
    fetch = [
        pltpu.make_async_copy(nbuf, nlist, lsem.at[0]),
        pltpu.make_async_copy(vbuf, vlist, lsem.at[1]),
    ]
    for copy in fetch:
        copy.start()
    key = lax.broadcasted_iota(jnp.int32, (nkeys, nkeys), 0)
    who = ((key % nz) * 2 + key // (nkeys // 2)) * agents + (key // nz) % agents
    order = (who == lax.broadcasted_iota(jnp.int32, (nkeys, nkeys), 1)).astype(F32).astype(BF16)
    lane_row = lax.broadcasted_iota(jnp.int32, (LANES, nkeys), 0) == HEAD_DIM
    unit = (lax.broadcasted_iota(jnp.int32, (nkeys, LANES), 1) == HEAD_DIM).astype(F32)
    for i in range(nt):
        row = jnp.where(lane_row, abuf[i].astype(F32), 0.0).astype(BF16)
        bias_v[i] = ((mm_t(order, row) - unit) * (-NEG)).astype(BF16).reshape(bias_v.shape[1:])

    weight(3).wait()
    weight(4).wait()

    def unpack(side, part):
        low = low_lanes(half)

        def body(i, carry):
            for k in range(KV_HEADS):
                both = kvb[side, part, i, k].astype(F32)
                at = 2 * side + part
                keys_v[i, k, at] = jnp.where(low, both, bias_v[i, at].astype(F32)).astype(BF16)
                values_v[i, k, at] = jnp.where(low, 1.0, both).astype(BF16)
            return carry

        lax.fori_loop(0, nt, body, 0)

    def swap(part):
        return pltpu.make_async_remote_copy(
            src_ref=kvb.at[core, part],
            dst_ref=kvb.at[core, part],
            send_sem=ksend.at[part],
            recv_sem=krecv.at[part],
            device_id=partner,
            device_id_type=MESH,
        )

    for h in range(agents):
        landed = rbuf1.at[h, pl.ds(0, steps - 1)]
        with scope(f"RWAIT{h}"):
            pltpu.make_async_copy(landed, landed, recv1.at[h]).wait()
        spread[pl.ds(0, steps * QTILES), :] = rbuf1[h].astype(F32).reshape(steps * QTILES, LANES)
        state = jnp.concatenate(
            [spread[pl.ds(q, steps, stride=QTILES), :] for q in range(QTILES)], axis=1
        )
        normed = normalize(state, gain2_ref[...])
        rows = pl.ds(h * steps, steps)
        kv = mm(normed, wkv2[...])
        for k in range(KV_HEADS):
            kvf[k, rows, :] = pack_keyval(kv, k)
        if h % 2 == 1:
            part = h // 2

            def place(i, carry):
                for k in range(KV_HEADS):
                    kvb[core, part, i, k] = jnp.concatenate(
                        [
                            kvf[k, pl.ds(pl.multiple_of(a * steps + i * nz, nz), nz), :]
                            for a in (h - 1, h)
                        ],
                        axis=0,
                    ).astype(BF16)
                return carry

            lax.fori_loop(0, nt, place, 0)
            swap(part).start()
        q2buf[rows, :] = mm(normed, wq2[...])
        if h % 2 == 1:
            unpack(core, part)
    for part in range(2):
        with scope(f"SWAP{part}"):
            swap(part).wait()
        with scope("UNP"):
            unpack(1 - core, part)
    with scope("FETCH"):
        for copy in fetch:
            copy.wait()

    arows = agents * nz
    brows = agents * QTILES
    per_phase = nt // PHASES
    unit_a = (lax.broadcasted_iota(jnp.int32, (arows, LANES), 1) == HEAD_DIM).astype(F32)
    low_a = low_lanes(arows)

    def rows_of(i):
        return jnp.concatenate(
            [
                q2buf[pl.ds(pl.multiple_of(a * steps + i * nz, nz), nz), :]
                for a in range(agents)
            ],
            axis=0,
        )

    def list_of(i):
        return [jnp.where(vlist[i, 0, n] > 0, nlist[i, 0, n], nt) for n in range(nbrs)]

    def score(queries, listed, k):
        keys = jnp.concatenate([keys_v[n, k].reshape(nkeys, LANES) for n in listed], axis=0)
        return mm_t(stack_queries(queries[:, k * 256 : (k + 1) * 256], unit_a), keys)

    def mix(scores, listed, k):
        values = jnp.concatenate([values_v[n, k].reshape(nkeys, LANES) for n in listed], axis=0)
        top = jnp.maximum(jnp.max(scores, axis=1, keepdims=True), -1e29)
        mixed = mm(jnp.exp(scores - top).astype(BF16), values)
        for p in range(2):
            even = mixed[2 * p * arows : (2 * p + 1) * arows]
            odd_head = mixed[(2 * p + 1) * arows : (2 * p + 2) * arows]
            block = jnp.where(low_a, swap_halves(even), odd_head) * (
                1.0 / jnp.where(low_a, even, swap_halves(odd_head))
            )
            q = 2 * k + p
            for a in range(agents):
                spread2[pl.ds(q * agents + a, nz, stride=brows), :] = block[
                    a * nz : (a + 1) * nz
                ]

    def attend(tiles, phase):
        work = [
            (i, rows_of(i), list_of(i), k, places) for i, places in tiles for k in range(KV_HEADS)
        ]
        ahead = score(*work[0][1:4])
        for at, (i, _, listed, k, places) in enumerate(work):
            scores = ahead
            if at + 1 < len(work):
                ahead = score(*work[at + 1][1:4])
            mix(scores, listed, k)
            if k + 1 == KV_HEADS:
                sbuf2[i] = spread2[...].reshape(nz, brows, LANES).astype(BF16)
                for zz, tm in places:
                    pltpu.make_async_remote_copy(
                        src_ref=sbuf2.at[i, zz],
                        dst_ref=rbuf2.at[me],
                        send_sem=send2,
                        recv_sem=recv2.at[phase],
                        device_id=(i, tm),
                        device_id_type=MESH,
                    ).start()

    def tile_pair(n, carry):
        first, second = (jnp.bitwise_xor(t, far_tile(2 * n + j)) for j in range(2))
        attend([(first, spots), (second, spots)], 2 * n // per_phase)
        return carry

    def tile_single(n, carry):
        attend([(jnp.bitwise_xor(t, far_tile(n)), spots)], n)
        return carry

    with scope("ATT"):
        if per_phase % 2 == 0:
            lax.fori_loop(0, nt // 2 - 1, tile_pair, 0)
        else:
            lax.fori_loop(0, nt - 2, tile_single, 0)
    with scope("OWN"):
        if per_phase % 2 == 0:
            attend(
                [(jnp.bitwise_xor(t, far_tile(nt - 2)), spots), (t, spots[:-1])], PHASES - 1
            )
        else:
            attend([(jnp.bitwise_xor(t, far_tile(nt - 2)), spots)], PHASES - 2)
            attend([(t, spots[:-1])], PHASES - 1)
        rbuf2[me] = sbuf2[t, z]

    weight(5).wait()
    psteps = per_phase * nz
    results = []
    for phase in range(PHASES):
        count = psteps - (1 if phase == PHASES - 1 else 0)
        landed = rbuf2.at[pl.ds(0, count)]
        with scope(f"HWAIT{phase}"):
            pltpu.make_async_copy(landed, landed, recv2.at[phase]).wait()
        group = jnp.bitwise_xor(t // per_phase, (2, 1, 3, 0)[phase])
        at = pl.multiple_of(group * psteps, psteps)
        back = rbuf2[pl.ds(at, psteps)].astype(F32).reshape(psteps * brows, LANES)
        spread[pl.ds(0, psteps * brows), :] = back
        mixed = jnp.concatenate(
            [
                jnp.concatenate(
                    [
                        spread[pl.ds(q * agents + a, psteps, stride=brows), :]
                        for q in range(QTILES)
                    ],
                    axis=1,
                )
                for a in range(agents)
            ],
            axis=0,
        ).astype(BF16)
        projected = mm(mixed, wo2[...])
        for a in range(agents):
            here = pl.ds(pl.multiple_of(a * steps + at, psteps), psteps)
            out_v[here, :] = (
                mid_v[here, :].astype(F32) + projected[a * psteps : (a + 1) * psteps]
            ).astype(BF16)
            result = pltpu.make_async_copy(
                out_v.at[here], out_hbm.at[here], out_sem.at[phase * agents + a]
            )
            result.start()
            results.append(result)

    with scope("FIN"):
        for result in results:
            result.wait()
    for i, dst in enumerate((nbuf, vbuf, abuf)):
        others = dst.at[pl.ds(0, nt - 1)]
        pltpu.make_async_copy(others, others, isend.at[i]).wait()
    for h in range(agents):
        gone = sbuf1.at[h, pl.ds(0, steps - 1)]
        pltpu.make_async_copy(gone, gone, send1.at[h]).wait()
    gone = rbuf2.at[pl.ds(0, steps - 1)]
    pltpu.make_async_copy(gone, gone, send2).wait()


def per_device(
    nt,
    nz,
    histories,
    gain_time,
    wq_time,
    wkv_time,
    wo_time,
    gain_space,
    wq_space,
    wkv_space,
    wo_space,
    neighbours,
    nbr_valid,
    agent_valid,
):
    _, agents, steps, _ = histories.shape
    nbrs = neighbours.shape[1]
    half = agents // 2 * nz
    brows = agents * QTILES
    vmem = pl.BlockSpec(memory_space=pltpu.VMEM)
    hbm = pl.BlockSpec(memory_space=pl.ANY)
    dma = pltpu.SemaphoreType.DMA
    out = pl.pallas_call(
        functools.partial(kernel, (nt, nz, agents, nbrs)),
        out_shape=jax.ShapeDtypeStruct((agents * steps, D), BF16),
        in_specs=[hbm, vmem, vmem] + [hbm] * 9,
        out_specs=hbm,
        scratch_shapes=[
            pltpu.VMEM((agents * steps, D), BF16),
            pltpu.VMEM((D, D), BF16),
            pltpu.VMEM((D, 512), BF16),
            pltpu.VMEM((D, D), BF16),
            pltpu.VMEM((D, D), BF16),
            pltpu.VMEM((D, 512), BF16),
            pltpu.VMEM((D, D), BF16),
            pltpu.VMEM((agents * steps, D), BF16),
            pltpu.VMEM((steps, D), F32),
            pltpu.VMEM((steps, D), BF16),
            pltpu.VMEM((max(steps * QTILES, nt // PHASES * nz * brows), LANES), F32),
            pltpu.VMEM((agents, steps, QTILES, LANES), BF16),
            pltpu.VMEM((agents, steps, QTILES, LANES), BF16),
            pltpu.VMEM((agents * steps, D), F32),
            pltpu.VMEM((KV_HEADS, agents * steps, LANES), F32),
            pltpu.VMEM((2, 2, nt, KV_HEADS, half, LANES), BF16),
            pltpu.VMEM((nt + 1, KV_HEADS, 4, half, LANES), BF16),
            pltpu.VMEM((nt + 1, KV_HEADS, 4, half, LANES), BF16),
            pltpu.VMEM((nt, 4, half, LANES), BF16),
            pltpu.VMEM((nt, 1, nbrs), jnp.int32),
            pltpu.VMEM((nt, 1, nbrs), jnp.int32),
            pltpu.VMEM((nt, 1, 4 * half), jnp.int32),
            pltpu.SMEM((nt, 1, nbrs), jnp.int32),
            pltpu.SMEM((nt, 1, nbrs), jnp.int32),
            pltpu.VMEM((nz * brows, LANES), F32),
            pltpu.VMEM((nt, nz, brows, LANES), BF16),
            pltpu.VMEM((steps, brows, LANES), BF16),
            dma((6,)),
            dma((agents,)),
            dma((3,)),
            dma((3,)),
            dma((3,)),
            dma((agents,)),
            dma((agents,)),
            dma((2,)),
            dma((2,)),
            dma,
            dma((PHASES,)),
            dma((2,)),
            pltpu.VMEM((agents * steps, D), BF16),
            dma((PHASES * agents,)),
        ],
        compiler_params=pltpu.CompilerParams(
            collective_id=0, has_side_effects=True, vmem_limit_bytes=60 * 1024 * 1024
        ),
    )(
        histories.reshape(agents * steps, D),
        gain_time.reshape(1, D),
        gain_space.reshape(1, D),
        neighbours,
        nbr_valid,
        agent_valid,
        wq_time,
        wkv_time,
        wo_time,
        wq_space,
        wkv_space,
        wo_space,
    )
    return out.reshape(1, agents, steps, D)


def solution(mesh):
    return jax.shard_map(
        functools.partial(per_device, mesh.shape["tile"], mesh.shape["tm"] // 2),
        mesh=mesh,
        in_specs=(
            P("tile", "tm", None, None),
            P(),
            P(),
            P(),
            P(),
            P(),
            P(),
            P(),
            P(),
            P("tile", None),
            P("tile", None),
            P("tile", None),
        ),
        out_specs=P("tile", "tm", None, None),
        check_vma=False,
    )
```

```python
import contextlib
import functools

import jax
import jax.numpy as jnp
from jax import lax
from jax.experimental import pallas as pl
from jax.experimental.pallas import tpu as pltpu
from jax.sharding import PartitionSpec as P

HEADS = 16
KV_HEADS = 4
HEAD_DIM = 64
D = 1024
LANES = 128
QTILES = D // LANES
MESH = pl.DeviceIdType.MESH
BF16 = jnp.bfloat16
F32 = jnp.float32
NEG = -1e30


def scope(name):
    return contextlib.nullcontext()


def normalize(wide, gain):
    meansq = jnp.mean(wide * wide, axis=-1, keepdims=True)
    return (wide * lax.rsqrt(meansq + 1e-05) * gain).astype(BF16)


def mm(a, b):
    return jnp.dot(a, b, preferred_element_type=F32)


def mm_t(a, b):
    return lax.dot_general(a, b, (((1,), (1,)), ((), ())), preferred_element_type=F32)


def phases_of(nt):
    if nt == 16:
        return [(0, 4), (4, 4), (8, 4), (12, 2), (14, 2)]
    return [(i, 1) for i in range(nt)]


def low_lanes(rows):
    return lax.broadcasted_iota(jnp.int32, (rows, LANES), 1) < HEAD_DIM


def swap_halves(x):
    return pltpu.roll(x, HEAD_DIM, 1)


def pack_keyval(kv, k):
    at = (k // 2) * LANES
    keys = kv[:, at : at + LANES]
    values = kv[:, 2 * LANES + at : 3 * LANES + at]
    low = low_lanes(kv.shape[0])
    if k % 2 == 0:
        return jnp.where(low, keys, swap_halves(values))
    return jnp.where(low, swap_halves(keys), values)


def stack_queries(block, rest):
    low = low_lanes(block.shape[0])
    parts = []
    for pair in range(2):
        half = block[:, pair * LANES : (pair + 1) * LANES] * 0.125
        parts.append(jnp.where(low, half, rest))
        parts.append(jnp.where(low, swap_halves(half), rest))
    return jnp.concatenate(parts, axis=0).astype(BF16)


def merge_heads(out, rows):
    low = low_lanes(rows)
    parts = [out[g * rows : (g + 1) * rows] for g in range(4)]
    return [jnp.where(low, swap_halves(parts[2 * p]), parts[2 * p + 1]) for p in range(2)]


def kernel(
    dims,
    hist_hbm,
    gain1_hbm,
    gain2_hbm,
    neigh_ref,
    valid_ref,
    alive_ref,
    wq1_hbm,
    wkv1_hbm,
    wo1_hbm,
    wq2_hbm,
    wkv2_hbm,
    wo2_hbm,
    out_hbm,
    hist_v,
    wq1,
    wkv1,
    wo1,
    wq2,
    wkv2,
    wo2,
    mid_v,
    q1buf,
    tmix,
    spread,
    sbuf1,
    rbuf1,
    q2buf,
    kvf,
    kvb,
    keys_v,
    values_v,
    bias_v,
    nbuf,
    vbuf,
    abuf,
    nlist,
    vlist,
    spread2,
    sbuf2,
    rbuf2,
    w_sem,
    h_sem,
    isend,
    irecv,
    own_sem,
    send1,
    recv1,
    ksend,
    krecv,
    send2,
    recv2,
    lsem,
    out_v,
    out_sem,
    gain1_ref,
    gain2_ref,
    gain_sem,
):
    nt, nz, agents, nbrs = dims
    steps = nt * nz
    half = agents // 2 * nz
    t = lax.axis_index("tile")
    m = lax.axis_index("tm")
    z, core = m // 2, m % 2
    me = t * nz + z
    partner = (t, z * 2 + (1 - core))

    def history(a):
        rows = pl.ds(a * steps, steps)
        return pltpu.make_async_copy(hist_hbm.at[rows], hist_v.at[rows], h_sem.at[a])

    def weight(i):
        src, dst = (
            (wq1_hbm, wq1),
            (wkv1_hbm, wkv1),
            (wo1_hbm, wo1),
            (wq2_hbm, wq2),
            (wkv2_hbm, wkv2),
            (wo2_hbm, wo2),
        )[i]
        return pltpu.make_async_copy(src, dst, w_sem.at[i])

    gains = [
        pltpu.make_async_copy(gain1_hbm, gain1_ref, gain_sem.at[0]),
        pltpu.make_async_copy(gain2_hbm, gain2_ref, gain_sem.at[1]),
    ]
    gains[0].start()
    history(0).start()
    weight(1).start()
    weight(0).start()

    barrier = pltpu.get_barrier_semaphore()

    spots = []
    for r in range(nz):
        k = (r + 1) // 2
        dz = (nz // 2 - k if r % 2 == 1 else nz // 2 + k) % nz
        zz = jnp.bitwise_and(z + dz, nz - 1)
        spots.append((zz, zz * 2 + core))

    def far_four(n):
        return jnp.where(n < 2, n + 2, 3 - n)

    def far_tile(n):
        if nt != 16:
            return far_four(n)
        high = jnp.where(n < 4, 2, jnp.where(n < 8, 1, jnp.where(n < 12, 3, 0)))
        return high * 4 + far_four(jnp.bitwise_and(n, 3))

    def each_peer(act):
        def body(n, carry):
            tt = jnp.bitwise_xor(t, far_tile(n))
            for zz, tm in spots:
                act(tt, zz, tm)
            return carry

        lax.fori_loop(0, nt - 1, body, 0)
        for zz, tm in spots[:-1]:
            act(t, zz, tm)

    parity = jnp.bitwise_and(jnp.bitwise_xor(jnp.bitwise_xor(t, t // 4), z), 1)
    evens = (10, 2, 8, 5, 7, 13, 15, 0) if nt == 16 else (2, 0)

    def each_of_group(group, act):
        flip = parity if group == 0 else 1 - parity
        places = [[], []]
        for r in range(nz // 2):
            k = (r + 1) // 2
            away = (nz // 4 - k if r % 2 == 1 else nz // 4 + k) * 2 % nz
            for side, shift in enumerate((flip, 1 - flip)):
                zz = jnp.bitwise_and(z + shift + away, nz - 1)
                places[side].append((zz, zz * 2 + core))

        def body(n, carry):
            j = 0
            for at, even in enumerate(evens[:-1]):
                j = jnp.where(n == at, even, j)
            tt = jnp.bitwise_xor(t, j)
            for zz, tm in places[0]:
                act(tt, zz, tm)
            tt = jnp.bitwise_xor(tt, 1)
            for zz, tm in places[1]:
                act(tt, zz, tm)
            return carry

        lax.fori_loop(0, len(evens) - 1, body, 0)
        for zz, tm in places[1]:
            act(jnp.bitwise_xor(t, 1), zz, tm)
        for zz, tm in places[0][:-1]:
            act(t, zz, tm)

        @pl.when(flip == 1)
        def _():
            act(t, *places[0][-1])

    each_peer(
        lambda tt, zz, tm: pl.semaphore_signal(
            barrier, inc=1, device_id=(tt, tm), device_id_type=MESH
        )
    )
    pl.semaphore_signal(barrier, inc=1, device_id=partner, device_id_type=MESH)

    weight(2).start()
    for a in range(1, agents):
        history(a).start()

    own = [
        pltpu.make_async_copy(src, dst.at[t], own_sem.at[i])
        for i, (src, dst) in enumerate(
            ((neigh_ref, nbuf), (valid_ref, vbuf), (alive_ref, abuf))
        )
    ]

    causal = lax.broadcasted_iota(jnp.int32, (steps, steps), 0) >= lax.broadcasted_iota(
        jnp.int32, (steps, steps), 1
    )
    causal4 = jnp.concatenate([causal] * 4, axis=0)

    def temporal(h):
        rows = pl.ds(h * steps, steps)
        with scope(f"HISTW{h}"):
            history(h).wait()
            if h == 0:
                gains[0].wait()
                gains[1].start()
        normed = normalize(hist_v[rows, :].astype(F32), gain1_ref[...])
        if h == 0:
            with scope("W1"):
                weight(1).wait()
        kv = mm(normed, wkv1[...])
        if h == 0:
            with scope("W0"):
                weight(0).wait()
        q1buf[...] = mm(normed, wq1[...])
        if h == 0:
            for i in range(3, 6):
                weight(i).start()
        for k in range(KV_HEADS):
            keyval = pack_keyval(kv, k).astype(BF16)
            queries = stack_queries(q1buf[:, k * 256 : (k + 1) * 256], 0.0)
            scores = jnp.where(causal4, mm_t(queries, keyval), NEG)
            top = jnp.max(scores, axis=1, keepdims=True)
            expd = jnp.exp(scores - top)
            total = jnp.sum(expd, axis=1, keepdims=True)
            probs = (expd * (1.0 / total)).astype(BF16)
            mixed = merge_heads(mm(probs, keyval), steps)
            for p in range(2):
                at = (2 * k + p) * LANES
                tmix[:, at : at + LANES] = mixed[p].astype(BF16)
        if h == 0:
            with scope("W2"):
                weight(2).wait()
        mid = hist_v[rows, :].astype(F32) + mm(tmix[...], wo1[...])
        mid_v[rows, :] = mid.astype(BF16)
        for q in range(QTILES):
            spread[pl.ds(q, steps, stride=QTILES), :] = mid[:, q * LANES : (q + 1) * LANES]
        sbuf1[h] = spread[pl.ds(0, steps * QTILES), :].reshape(steps, QTILES, LANES).astype(BF16)
        rbuf1[h, me] = sbuf1[h, me]

    def send_chunk(h, group):
        each_of_group(
            group,
            lambda tt, zz, tm: pltpu.make_async_remote_copy(
                src_ref=sbuf1.at[h, tt * nz + zz],
                dst_ref=rbuf1.at[h, me],
                send_sem=send1.at[h],
                recv_sem=recv1.at[h],
                device_id=(tt, tm),
                device_id_type=MESH,
            ).start(),
        )

    def send_lists(r, carry):
        for i, (src, dst) in enumerate(
            ((neigh_ref, nbuf), (valid_ref, vbuf), (alive_ref, abuf))
        ):
            pltpu.make_async_remote_copy(
                src_ref=src,
                dst_ref=dst.at[t],
                send_sem=isend.at[i],
                recv_sem=irecv.at[i],
                device_id=(jnp.bitwise_xor(t, r), m),
                device_id_type=MESH,
            ).start()
        return carry

    for h in range(agents):
        with scope(f"TEMP{h}"):
            temporal(h)
        if h == 0:
            with scope("BARR"):
                pl.semaphore_wait(barrier, steps)
        with scope(f"SEND{h}"):
            send_chunk(h, 0)
            if h == 0:
                for copy in own:
                    copy.start()
                lax.fori_loop(1, nt, send_lists, 0)
    with scope("SENDB"):
        for h in range(agents):
            send_chunk(h, 1)

    nkeys = 2 * agents * nz
    keys_v[nt] = jnp.where(
        lax.broadcasted_iota(jnp.int32, (nkeys, LANES), 1) == HEAD_DIM, NEG, 0.0
    ).astype(BF16)[None].reshape(1, 4, nkeys // 4, LANES) + jnp.zeros(keys_v.shape[1:], BF16)
    values_v[nt] = jnp.zeros(values_v.shape[1:], BF16)
    with scope("IWAIT"):
        for copy in own:
            copy.wait()
        for i, dst in enumerate((nbuf, vbuf, abuf)):
            others = dst.at[pl.ds(0, nt - 1)]
            pltpu.make_async_copy(others, others, irecv.at[i]).wait()
    fetch = [
        pltpu.make_async_copy(nbuf, nlist, lsem.at[0]),
        pltpu.make_async_copy(vbuf, vlist, lsem.at[1]),
    ]
    for copy in fetch:
        copy.start()
    key = lax.broadcasted_iota(jnp.int32, (nkeys, nkeys), 0)
    who = ((key % nz) * 2 + key // (nkeys // 2)) * agents + (key // nz) % agents
    order = (who == lax.broadcasted_iota(jnp.int32, (nkeys, nkeys), 1)).astype(F32).astype(BF16)
    lane_row = lax.broadcasted_iota(jnp.int32, (LANES, nkeys), 0) == HEAD_DIM
    unit = (lax.broadcasted_iota(jnp.int32, (nkeys, LANES), 1) == HEAD_DIM).astype(F32)
    for i in range(nt):
        row = jnp.where(lane_row, abuf[i].astype(F32), 0.0).astype(BF16)
        bias_v[i] = ((mm_t(order, row) - unit) * (-NEG)).astype(BF16).reshape(bias_v.shape[1:])

    weight(3).wait()
    weight(4).wait()
    gains[1].wait()

    def unpack(side, part):
        low = low_lanes(half)

        def body(i, carry):
            for k in range(KV_HEADS):
                both = kvb[side, part, i, k].astype(F32)
                at = 2 * side + part
                keys_v[i, k, at] = jnp.where(low, both, bias_v[i, at].astype(F32)).astype(BF16)
                values_v[i, k, at] = jnp.where(low, 1.0, both).astype(BF16)
            return carry

        lax.fori_loop(0, nt, body, 0)

    def swap(part):
        return pltpu.make_async_remote_copy(
            src_ref=kvb.at[core, part],
            dst_ref=kvb.at[core, part],
            send_sem=ksend.at[part],
            recv_sem=krecv.at[part],
            device_id=partner,
            device_id_type=MESH,
        )

    for h in range(agents):
        landed = rbuf1.at[h, pl.ds(0, steps - 1)]
        with scope(f"RWAIT{h}"):
            pltpu.make_async_copy(landed, landed, recv1.at[h]).wait()
        spread[pl.ds(0, steps * QTILES), :] = rbuf1[h].astype(F32).reshape(steps * QTILES, LANES)
        state = jnp.concatenate(
            [spread[pl.ds(q, steps, stride=QTILES), :] for q in range(QTILES)], axis=1
        )
        normed = normalize(state, gain2_ref[...])
        rows = pl.ds(h * steps, steps)
        kv = mm(normed, wkv2[...])
        for k in range(KV_HEADS):
            kvf[k, rows, :] = pack_keyval(kv, k)
        if h % 2 == 1:
            part = h // 2

            def place(i, carry):
                for k in range(KV_HEADS):
                    kvb[core, part, i, k] = jnp.concatenate(
                        [
                            kvf[k, pl.ds(pl.multiple_of(a * steps + i * nz, nz), nz), :]
                            for a in (h - 1, h)
                        ],
                        axis=0,
                    ).astype(BF16)
                return carry

            lax.fori_loop(0, nt, place, 0)
            swap(part).start()
        q2buf[rows, :] = mm(normed, wq2[...])
        if h % 2 == 1:
            unpack(core, part)
    for part in range(2):
        with scope(f"SWAP{part}"):
            swap(part).wait()
        with scope("UNP"):
            unpack(1 - core, part)
    with scope("FETCH"):
        for copy in fetch:
            copy.wait()

    arows = agents * nz
    brows = agents * QTILES
    unit_a = (lax.broadcasted_iota(jnp.int32, (arows, LANES), 1) == HEAD_DIM).astype(F32)
    low_a = low_lanes(arows)

    def rows_of(i):
        return jnp.concatenate(
            [
                q2buf[pl.ds(pl.multiple_of(a * steps + i * nz, nz), nz), :]
                for a in range(agents)
            ],
            axis=0,
        )

    def list_of(i):
        return [jnp.where(vlist[i, 0, n] > 0, nlist[i, 0, n], nt) for n in range(nbrs)]

    def score(queries, listed, k):
        keys = jnp.concatenate([keys_v[n, k].reshape(nkeys, LANES) for n in listed], axis=0)
        return mm_t(stack_queries(queries[:, k * 256 : (k + 1) * 256], unit_a), keys)

    def mix(scores, listed, k):
        values = jnp.concatenate([values_v[n, k].reshape(nkeys, LANES) for n in listed], axis=0)
        top = jnp.maximum(jnp.max(scores, axis=1, keepdims=True), -1e29)
        mixed = mm(jnp.exp(scores - top).astype(BF16), values)
        for p in range(2):
            even = mixed[2 * p * arows : (2 * p + 1) * arows]
            odd_head = mixed[(2 * p + 1) * arows : (2 * p + 2) * arows]
            block = jnp.where(low_a, swap_halves(even), odd_head) * (
                1.0 / jnp.where(low_a, even, swap_halves(odd_head))
            )
            q = 2 * k + p
            for a in range(agents):
                spread2[pl.ds(q * agents + a, nz, stride=brows), :] = block[
                    a * nz : (a + 1) * nz
                ]

    def attend(tiles, phase):
        work = [
            (i, rows_of(i), list_of(i), k, places) for i, places in tiles for k in range(KV_HEADS)
        ]
        ahead = score(*work[0][1:4])
        for at, (i, _, listed, k, places) in enumerate(work):
            scores = ahead
            if at + 1 < len(work):
                ahead = score(*work[at + 1][1:4])
            mix(scores, listed, k)
            if k + 1 == KV_HEADS:
                sbuf2[i] = spread2[...].reshape(nz, brows, LANES).astype(BF16)
                for zz, tm in places:
                    pltpu.make_async_remote_copy(
                        src_ref=sbuf2.at[i, zz],
                        dst_ref=rbuf2.at[me],
                        send_sem=send2,
                        recv_sem=recv2.at[phase],
                        device_id=(i, tm),
                        device_id_type=MESH,
                    ).start()

    def tile_pair(n, carry):
        first, second = (jnp.bitwise_xor(t, far_tile(2 * n + j)) for j in range(2))
        attend([(first, spots), (second, spots)], n // 2)
        return carry

    def tile_single(n, carry):
        attend([(jnp.bitwise_xor(t, far_tile(n)), spots)], n)
        return carry

    with scope("ATT"):
        if nt == 16:
            lax.fori_loop(0, nt // 2 - 1, tile_pair, 0)
        else:
            lax.fori_loop(0, nt - 2, tile_single, 0)
    with scope("OWN"):
        if nt == 16:
            attend([(jnp.bitwise_xor(t, far_tile(nt - 2)), spots), (t, spots[:-1])], 4)
        else:
            attend([(jnp.bitwise_xor(t, far_tile(nt - 2)), spots)], nt - 2)
            attend([(t, spots[:-1])], nt - 1)
        rbuf2[me] = sbuf2[t, z]

    weight(5).wait()
    results = []
    for phase, (start, count) in enumerate(phases_of(nt)):
        psteps = count * nz
        count = psteps - (1 if start + count == nt else 0)
        landed = rbuf2.at[pl.ds(0, count)]
        with scope(f"HWAIT{phase}"):
            pltpu.make_async_copy(landed, landed, recv2.at[phase]).wait()
        group = jnp.bitwise_xor(t, far_tile(start)) // (psteps // nz)
        at = pl.multiple_of(group * psteps, psteps)
        back = rbuf2[pl.ds(at, psteps)].astype(F32).reshape(psteps * brows, LANES)
        spread[pl.ds(0, psteps * brows), :] = back
        mixed = jnp.concatenate(
            [
                jnp.concatenate(
                    [
                        spread[pl.ds(q * agents + a, psteps, stride=brows), :]
                        for q in range(QTILES)
                    ],
                    axis=1,
                )
                for a in range(agents)
            ],
            axis=0,
        ).astype(BF16)
        projected = mm(mixed, wo2[...])
        for a in range(agents):
            here = pl.ds(pl.multiple_of(a * steps + at, psteps), psteps)
            out_v[here, :] = (
                mid_v[here, :].astype(F32) + projected[a * psteps : (a + 1) * psteps]
            ).astype(BF16)
            result = pltpu.make_async_copy(
                out_v.at[here], out_hbm.at[here], out_sem.at[phase * agents + a]
            )
            result.start()
            results.append(result)

    with scope("FIN"):
        for result in results:
            result.wait()
    for i, dst in enumerate((nbuf, vbuf, abuf)):
        others = dst.at[pl.ds(0, nt - 1)]
        pltpu.make_async_copy(others, others, isend.at[i]).wait()
    for h in range(agents):
        gone = sbuf1.at[h, pl.ds(0, steps - 1)]
        pltpu.make_async_copy(gone, gone, send1.at[h]).wait()
    gone = rbuf2.at[pl.ds(0, steps - 1)]
    pltpu.make_async_copy(gone, gone, send2).wait()


def hand_over(src, dst, buf, in_sem, out_sem):
    parts = in_sem.shape[0]
    rows = src.shape[0] // parts
    spans = [pl.ds(i * rows, rows) for i in range(parts)]
    reads = [
        pltpu.make_async_copy(src.at[at], buf.at[at], in_sem.at[i]) for i, at in enumerate(spans)
    ]
    writes = [
        pltpu.make_async_copy(buf.at[at], dst.at[at], out_sem.at[i]) for i, at in enumerate(spans)
    ]
    for read in reads:
        read.start()
    for read, write in zip(reads, writes):
        read.wait()
        write.start()
    for write in writes:
        write.wait()


def per_device(
    nt,
    nz,
    histories,
    gain_time,
    wq_time,
    wkv_time,
    wo_time,
    gain_space,
    wq_space,
    wkv_space,
    wo_space,
    neighbours,
    nbr_valid,
    agent_valid,
):
    _, agents, steps, _ = histories.shape
    nbrs = neighbours.shape[1]
    half = agents // 2 * nz
    brows = agents * QTILES
    hbm = pl.BlockSpec(memory_space=pl.ANY)
    dma = pltpu.SemaphoreType.DMA
    out = pl.pallas_call(
        functools.partial(kernel, (nt, nz, agents, nbrs)),
        out_shape=jax.ShapeDtypeStruct((agents * steps, D), BF16),
        in_specs=[hbm] * 12,
        out_specs=hbm,
        scratch_shapes=[
            pltpu.VMEM((agents * steps, D), BF16),
            pltpu.VMEM((D, D), BF16),
            pltpu.VMEM((D, 512), BF16),
            pltpu.VMEM((D, D), BF16),
            pltpu.VMEM((D, D), BF16),
            pltpu.VMEM((D, 512), BF16),
            pltpu.VMEM((D, D), BF16),
            pltpu.VMEM((agents * steps, D), BF16),
            pltpu.VMEM((steps, D), F32),
            pltpu.VMEM((steps, D), BF16),
            pltpu.VMEM((max(steps * QTILES, max(1, nt // 4) * nz * brows), LANES), F32),
            pltpu.VMEM((agents, steps, QTILES, LANES), BF16),
            pltpu.VMEM((agents, steps, QTILES, LANES), BF16),
            pltpu.VMEM((agents * steps, D), F32),
            pltpu.VMEM((KV_HEADS, agents * steps, LANES), F32),
            pltpu.VMEM((2, 2, nt, KV_HEADS, half, LANES), BF16),
            pltpu.VMEM((nt + 1, KV_HEADS, 4, half, LANES), BF16),
            pltpu.VMEM((nt + 1, KV_HEADS, 4, half, LANES), BF16),
            pltpu.VMEM((nt, 4, half, LANES), BF16),
            pltpu.VMEM((nt, 1, nbrs), jnp.int32),
            pltpu.VMEM((nt, 1, nbrs), jnp.int32),
            pltpu.VMEM((nt, 1, 4 * half), jnp.int32),
            pltpu.SMEM((nt, 1, nbrs), jnp.int32),
            pltpu.SMEM((nt, 1, nbrs), jnp.int32),
            pltpu.VMEM((nz * brows, LANES), F32),
            pltpu.VMEM((nt, nz, brows, LANES), BF16),
            pltpu.VMEM((steps, brows, LANES), BF16),
            dma((6,)),
            dma((agents,)),
            dma((3,)),
            dma((3,)),
            dma((3,)),
            dma((agents,)),
            dma((agents,)),
            dma((2,)),
            dma((2,)),
            dma,
            dma((len(phases_of(nt)),)),
            dma((2,)),
            pltpu.VMEM((agents * steps, D), BF16),
            dma((len(phases_of(nt)) * agents,)),
            pltpu.VMEM((1, D), F32),
            pltpu.VMEM((1, D), F32),
            dma((2,)),
        ],
        compiler_params=pltpu.CompilerParams(
            collective_id=0, has_side_effects=True, vmem_limit_bytes=60 * 1024 * 1024
        ),
    )(
        histories.reshape(agents * steps, D),
        gain_time.reshape(1, D),
        gain_space.reshape(1, D),
        neighbours,
        nbr_valid,
        agent_valid,
        wq_time,
        wkv_time,
        wo_time,
        wq_space,
        wkv_space,
        wo_space,
    )
    out = pl.pallas_call(
        hand_over,
        out_shape=jax.ShapeDtypeStruct(out.shape, BF16),
        in_specs=[hbm],
        out_specs=hbm,
        scratch_shapes=[pltpu.VMEM(out.shape, BF16), dma((8,)), dma((8,))],
        compiler_params=pltpu.CompilerParams(vmem_limit_bytes=60 * 1024 * 1024),
    )(out)
    return out.reshape(1, agents, steps, D)


def solution(mesh):
    return jax.shard_map(
        functools.partial(per_device, mesh.shape["tile"], mesh.shape["tm"] // 2),
        mesh=mesh,
        in_specs=(
            P("tile", "tm", None, None),
            P(),
            P(),
            P(),
            P(),
            P(),
            P(),
            P(),
            P(),
            P("tile", None),
            P("tile", None),
            P("tile", None),
        ),
        out_specs=P("tile", "tm", None, None),
        check_vma=False,
    )
```
